32 devices in a mesh: dp: 8 (over z, y), mp: 4 (over x, core).
Axes of the slice: x: 2, y: 2, z: 4, core: 2. Of those that a mesh axis runs over, the one named last changes fastest.
Arguments:
- hidden: bfloat16 [16, 64, 3584], P('dp', None, 'mp'), may hold values from -6 to 6
- rewards: float32 [16, 64], P('dp'), may hold values from -6 to 6
- actions: int32 [16, 64], P('dp'), may hold values from 0 to 152063, as said below
- lengths: int32 [16], P('dp'), may hold values from 1 to 64, 512 in all
- table: bfloat16 [152064, 3584], P('dp', 'mp'), may hold values from -0.09375 to 0.09375
- q_one: bfloat16 [3584, 3584], P('dp', 'mp'), may hold values from -0.09375 to 0.09375
- q_two: bfloat16 [3584, 3584], P('dp', 'mp'), may hold values from -0.09375 to 0.09375
- t_one: bfloat16 [3584, 3584], P('dp', 'mp'), may hold values from -0.09375 to 0.09375
- t_two: bfloat16 [3584, 3584], P('dp', 'mp'), may hold values from -0.09375 to 0.09375
- value_weight: bfloat16 [3584], P('mp'), may hold values from -0.09375 to 0.09375
- value_bias: float32 [1], replicated, may hold values from -3 to 3
Outputs:
- loss: float32 [], replicated
- grad_q_one: float32 [3584, 3584], P('dp', 'mp')
- grad_q_two: float32 [3584, 3584], P('dp', 'mp')
- grad_value: float32 [3584], P('mp')
- grad_bias: float32 [1], replicated
- target_one: bfloat16 [3584, 3584], P('dp', 'mp')
- target_two: bfloat16 [3584, 3584], P('dp', 'mp')
The draws below stay inside these ranges and needn't reach their ends.
Inputs may be any that keep to these rules, and one draw needn't show every extreme that they name: `actions`: among the 128 positions of the prompts of one index of dp, exactly 16 action ids fall in each of the aligned blocks of 19008 vocabulary rows.
All inputs are finite; a program needn't handle non-finite values. No bound on the sum of `lengths` on one device may be relied on, other than what follows from the above.
Results may differ from the reference program's by a relative error of at most 0.0045.
Values may be sent and summed in bfloat16 or wider, within the bound.
A program may use at most 192 MiB of HBM per device.

```python
import math
import jax
import jax.numpy as jnp
import numpy as np
from jax import lax

D = 3584
V = 152064
DH = 3584
PR_DEV = 2
SLOT = 64
PROMPTS = 16


def draw_actions(key, part):
    blocks = PROMPTS // PR_DEV
    per_block = PR_DEV * SLOT
    row_count = V // blocks
    keys_split = jax.random.split(jax.random.fold_in(key, 11), blocks)

    def shuffle(block_key):
        return jax.random.permutation(block_key, per_block)
    shuffled = jax.vmap(shuffle)(keys_split)
    holders = shuffled % blocks
    offsets = jax.random.randint(jax.random.fold_in(key, 12), (blocks, per_block), 0, row_count)
    return (holders * row_count + offsets).astype(jnp.int32).reshape(PROMPTS, SLOT)


def steps_of(key, shape, pieces, least, largest):
    factor_of = 1.0
    for dim, blocks in pieces:
        steps = jax.random.uniform(jax.random.fold_in(jax.random.fold_in(key, 6), dim), (blocks,), jnp.float32, least / len(pieces), largest / len(pieces))
        factor_of = factor_of * jnp.repeat(jnp.exp(steps), shape[dim] // blocks).reshape((-1,) + (1,) * (len(shape) - 1 - dim))
    return factor_of


def profile(count, total, most, lean):
    weights = [(1 << 20) // math.isqrt(grade ** lean) + 1 for grade in range(2, count + 1)]
    surplus, holding = total - most - (count - 1), [1] * (count - 1)
    while surplus > 0:
        candidates = [i for i in range(count - 1) if holding[i] < most]
        mass, left = sum([weights[i] for i in candidates]), surplus
        for i in candidates:
            more = min(most - holding[i], max(1, left * weights[i] // mass), surplus)
            holding[i] = holding[i] + more
            surplus = surplus - more
    return np.array([most] + holding)


def uneven_parts(own_key, count, total, limit, lean):
    if count == 2:
        one = jax.random.randint(own_key, (), max(1, total - limit), min(limit, total - 1) + 1)
        return jnp.stack([one, total - one])
    tallies = jnp.asarray(profile(count, total, limit, lean), jnp.int32)
    twos = (count - 1) // 2
    source_of, sink = tallies[1:1 + 2 * twos:2], tallies[2:2 + 2 * twos:2]
    slack = jnp.minimum(source_of - 1, limit - sink)
    moved = jax.random.randint(jax.random.fold_in(own_key, 1), (twos,), 0, 1 << 20) % (slack + 1)
    tallies = tallies.at[1:1 + 2 * twos:2].set(source_of - moved).at[2:2 + 2 * twos:2].set(sink + moved)
    return tallies[jax.random.permutation(jax.random.fold_in(own_key, 2), count)]


def scatter_about(key, shape, deviation, most, shards=(), kind=jnp.bfloat16):
    entries = deviation * jax.random.normal(key, shape, jnp.float32)
    if shards:
        entries = entries * steps_of(key, shape, shards, -0.22, 0.18)
    return jnp.clip(entries, -most, most).astype(kind)


def setup_inputs(seed: int = 0) -> dict:
    seeds = jax.random.split(jax.random.key(seed), 12)
    hidden = scatter_about(seeds[0], (PROMPTS, SLOT, D), 1.0, 6.0, ((0, 8), (2, 4)))
    rewards = scatter_about(seeds[1], (PROMPTS, SLOT), 1.0, 6.0, ((0, 8),), jnp.float32)
    actions = draw_actions(jax.random.fold_in(seeds[11], 71), 0)
    lengths = uneven_parts(seeds[3], PROMPTS, PROMPTS * SLOT // 2, SLOT, 2).astype(jnp.int32)
    table = scatter_about(seeds[4], (V, DH), DH ** -0.5, 0.09375, ((0, 8), (1, 4)))
    q_one = scatter_about(seeds[5], (D, DH), D ** -0.5, 0.09375, ((0, 8), (1, 4)))
    q_two = scatter_about(seeds[6], (D, DH), D ** -0.5, 0.09375, ((0, 8), (1, 4)))
    t_one = scatter_about(seeds[7], (D, DH), D ** -0.5, 0.09375, ((0, 8), (1, 4)))
    t_two = scatter_about(seeds[8], (D, DH), D ** -0.5, 0.09375, ((0, 8), (1, 4)))
    value_weight = scatter_about(seeds[9], (D,), D ** -0.5, 0.09375, ((0, 4),))
    value_bias = scatter_about(seeds[10], (1,), 1.0, 3.0, (), jnp.float32)
    return dict(hidden=hidden, rewards=rewards, actions=actions, lengths=lengths, table=table, q_one=q_one, q_two=q_two, t_one=t_one, t_two=t_two, value_weight=value_weight, value_bias=value_bias)


discount = 0.99
expectile = 0.7
polyak_rate = 0.005

def head_gelu(inputs):
    return jax.nn.gelu(inputs, approximate=True)

def slope(preact, upstream):
    _, pullback = jax.vjp(head_gelu, preact)
    return pullback(upstream)[0]

def critic_terms(q_first, q_second, t_first, t_second, values, rewards, lengths):
    positions = jnp.arange(values.shape[1], dtype=jnp.int32)[None, :]
    valid = positions < lengths[:, None]
    follows = positions + 1 < lengths[:, None]
    shifted = jnp.concatenate([values[:, 1:], jnp.zeros_like(values[:, :1])], axis=1)
    target = rewards + discount * jnp.where(follows, shifted, 0.0)
    lowest = jnp.minimum(t_first, t_second)
    spread = lowest - values
    weights = jnp.where(spread < 0.0, 1.0 - expectile, expectile)
    err_one = q_first - target
    err_two = q_second - target
    loss_sum = jnp.sum(jnp.where(valid, err_one * err_one + err_two * err_two + weights * spread * spread, 0.0))
    grad_first = jnp.where(valid, 2.0 * err_one, 0.0)
    grad_second = jnp.where(valid, 2.0 * err_two, 0.0)
    grad_values = jnp.where(valid, -2.0 * weights * spread, 0.0)
    return (grad_first, grad_second, grad_values, loss_sum)

def reference(hidden, rewards, actions, lengths, table, q_one, q_two, t_one, t_two, value_weight, value_bias):
    blocks = PROMPTS // PR_DEV
    total_count = jnp.sum(lengths).astype(jnp.float32)

    def one_block(carry, inputs):
        acc_one, acc_two, acc_value, acc_bias, acc_loss = carry
        block_hidden, block_rewards, block_actions, block_lengths = inputs
        flat = block_hidden.reshape(PR_DEV * SLOT, D)
        embed = table[block_actions.reshape(-1)].astype(jnp.float32)
        preacts = [jnp.dot(flat, weight, preferred_element_type=jnp.float32) for weight in (q_one, q_two, t_one, t_two)]
        scores = [lax.optimization_barrier(jnp.sum(head_gelu(preact) * embed, axis=1)).reshape(PR_DEV, SLOT) for preact in preacts]
        values = jnp.dot(flat, value_weight, preferred_element_type=jnp.float32).reshape(PR_DEV, SLOT) + value_bias[0]
        grad_first, grad_second, grad_values, loss_sum = critic_terms(scores[0], scores[1], scores[2], scores[3], values, block_rewards, block_lengths)
        back_one = slope(preacts[0], grad_first.reshape(-1, 1) * embed).astype(jnp.bfloat16)
        back_two = slope(preacts[1], grad_second.reshape(-1, 1) * embed).astype(jnp.bfloat16)
        dims = (((0,), (0,)), ((), ()))
        acc_one = acc_one + lax.dot_general(flat, back_one, dims, preferred_element_type=jnp.float32)
        acc_two = acc_two + lax.dot_general(flat, back_two, dims, preferred_element_type=jnp.float32)
        acc_value = acc_value + jnp.dot(grad_values.reshape(-1), flat.astype(jnp.float32), precision=lax.Precision.HIGHEST)
        acc_bias = acc_bias + jnp.sum(grad_values)
        acc_loss = acc_loss + loss_sum
        return ((acc_one, acc_two, acc_value, acc_bias, acc_loss), None)
    start = (jnp.zeros((D, DH), jnp.float32), jnp.zeros((D, DH), jnp.float32), jnp.zeros((D,), jnp.float32), jnp.zeros((), jnp.float32), jnp.zeros((), jnp.float32))
    inputs = (hidden.reshape(blocks, PR_DEV, SLOT, D), rewards.reshape(blocks, PR_DEV, SLOT), actions.reshape(blocks, PR_DEV, SLOT), lengths.reshape(blocks, PR_DEV))
    final, _ = lax.scan(one_block, start, inputs)
    acc_one, acc_two, acc_value, acc_bias, acc_loss = final
    new_one = ((1.0 - polyak_rate) * t_one.astype(jnp.float32) + polyak_rate * q_one.astype(jnp.float32)).astype(jnp.bfloat16)
    new_two = ((1.0 - polyak_rate) * t_two.astype(jnp.float32) + polyak_rate * q_two.astype(jnp.float32)).astype(jnp.bfloat16)
    return (acc_loss / total_count, acc_one / total_count, acc_two / total_count, acc_value / total_count, (acc_bias / total_count).reshape(1), new_one, new_two)
```

```python
import jax
import jax.numpy as jnp
from jax import lax
from jax.sharding import PartitionSpec as P

discount = 0.99
expectile = 0.7
polyak_rate = 0.005
f32 = jnp.float32
bf16 = jnp.bfloat16


def head_gelu(inputs):
    return jax.nn.gelu(inputs, approximate=True)


def slope(preact, upstream):
    _, pullback = jax.vjp(head_gelu, preact)
    return pullback(upstream)[0]


def pick(mask, row):
    return jnp.sum(jnp.where(mask, row[None, :], jnp.zeros((), row.dtype)), axis=1)


def on_device(
    hidden, rewards, actions, lengths, table, q_one, q_two, t_one, t_two, value_weight, value_bias
):
    dp = lax.axis_size("dp")
    me = lax.axis_index("dp")
    prompts, slots, width = hidden.shape
    own = prompts * slots
    total = own * dp
    packed = total // 2
    share = packed // dp
    cols = q_one.shape[1]
    rows = q_one.shape[0]
    local_rows = table.shape[0]
    local_flat = hidden.reshape(own, width)

    stacked = jnp.concatenate([local_flat, value_weight.reshape(1, width)], axis=0)
    wide = lax.all_gather(stacked, "mp", axis=1, tiled=True)
    flat, value_row = wide[:own], wide[own:]
    values = (
        jnp.sum(flat.astype(f32) * value_row.astype(f32), axis=1).reshape(prompts, slots)
        + value_bias[0]
    )
    positions = jnp.arange(slots, dtype=jnp.int32)[None, :]
    follows = positions + 1 < lengths[:, None]
    shifted = jnp.concatenate([values[:, 1:], jnp.zeros_like(values[:, :1])], axis=1)
    target = rewards + discount * jnp.where(follows, shifted, 0.0)

    ints = jnp.concatenate([actions, lengths[:, None]], axis=1)
    all_ints = lax.all_gather(ints, "dp", axis=0, tiled=True)
    all_lengths = all_ints[:, slots]
    ids = all_ints[:, :slots].reshape(total)
    facts = jnp.stack([target.reshape(own), values.reshape(own)])
    all_facts = lax.all_gather(facts, "dp", axis=1, tiled=True)
    count = jnp.sum(all_lengths).astype(f32)
    factor = 1.0 / count

    prompt_ids = jnp.arange(prompts * dp, dtype=jnp.int32)
    offsets = jnp.sum(
        jnp.where(prompt_ids[None, :] < prompt_ids[:, None], all_lengths[None, :], 0), axis=1
    )
    place = jnp.where(
        positions < all_lengths[:, None], offsets[:, None] + positions, -1
    ).reshape(total)
    own_slots = jnp.arange(share, dtype=jnp.int32)[:, None] + me * share
    own_mask = own_slots == place[None, :]

    holders = ids // local_rows
    by_source = holders.reshape(dp, own)
    order = jnp.arange(own, dtype=jnp.int32)
    earlier = (by_source[:, :, None] == by_source[:, None, :]) & (
        order[None, None, :] < order[None, :, None]
    )
    per_source = own // dp
    rank = (
        jnp.sum(earlier.astype(jnp.int32), axis=2)
        + jnp.arange(dp, dtype=jnp.int32)[:, None] * per_source
    ).reshape(total)
    where_held = holders * own + rank
    wanted = jnp.arange(own, dtype=jnp.int32)[:, None] + me * own == where_held[None, :]
    requests = pick(wanted, ids - me * local_rows)
    found = table[requests]
    all_found = lax.all_gather(found, "dp", axis=0, tiled=True)
    seat = pick(own_mask, where_held)
    seat_mask = (jnp.arange(total, dtype=jnp.int32)[None, :] == seat[:, None]).astype(bf16)
    embed = jnp.dot(seat_mask, all_found, preferred_element_type=f32)

    spread = lax.all_to_all(flat, "dp", split_axis=1, concat_axis=0, tiled=True)
    pack_mask = (jnp.arange(packed, dtype=jnp.int32)[:, None] == place[None, :]).astype(bf16)
    held = jnp.dot(pack_mask, spread, preferred_element_type=f32).astype(bf16)

    partial = jnp.concatenate(
        [
            jnp.dot(held, weight, preferred_element_type=f32).astype(bf16)
            for weight in (q_one, q_two, t_one, t_two)
        ],
        axis=1,
    )
    swapped = lax.all_to_all(partial, "dp", split_axis=0, concat_axis=0, tiled=True)
    pre = jnp.sum(swapped.reshape(dp, share, 4 * cols).astype(f32), axis=0)
    pres = [pre[:, k * cols : (k + 1) * cols] for k in range(4)]
    scores = jnp.stack([jnp.sum(head_gelu(p) * embed, axis=1) for p in pres])
    board = lax.dynamic_update_slice(
        jnp.zeros((4, packed), f32), scores, (jnp.zeros((), jnp.int32), me * share)
    )
    all_scores = lax.psum(board, ("dp", "mp"))

    pack_bool = jnp.arange(packed, dtype=jnp.int32)[:, None] == place[None, :]
    goal = pick(pack_bool, all_facts[0])
    worth = pick(pack_bool, all_facts[1])
    lowest = jnp.minimum(all_scores[2], all_scores[3])
    spread_to = lowest - worth
    weights = jnp.where(spread_to < 0.0, 1.0 - expectile, expectile)
    err_one = all_scores[0] - goal
    err_two = all_scores[1] - goal
    loss = (
        jnp.sum(err_one * err_one + err_two * err_two + weights * spread_to * spread_to) * factor
    )
    grad_values = -2.0 * weights * spread_to
    bias_grad = jnp.sum(grad_values) * factor

    up_one = lax.dynamic_slice(2.0 * err_one, (me * share,), (share,))
    up_two = lax.dynamic_slice(2.0 * err_two, (me * share,), (share,))
    back = jnp.concatenate(
        [
            slope(pres[0], up_one[:, None] * embed).astype(bf16),
            slope(pres[1], up_two[:, None] * embed).astype(bf16),
        ],
        axis=1,
    )
    all_back = lax.all_gather(back, "dp", axis=0, tiled=True)
    dims = (((0,), (0,)), ((), ()))
    head_one = (
        lax.dot_general(held, all_back[:, :cols], dims, preferred_element_type=f32) * factor
    )
    head_two = (
        lax.dot_general(held, all_back[:, cols:], dims, preferred_element_type=f32) * factor
    )

    own_place = lax.dynamic_slice(place, (me * own,), (own,))
    own_errors = pick(
        own_place[:, None] == jnp.arange(packed, dtype=jnp.int32)[None, :], grad_values
    )
    value_part = jnp.sum(own_errors[:, None] * local_flat.astype(f32), axis=0)
    value_grad = lax.psum(value_part * factor, "dp")
    new_one = ((1.0 - polyak_rate) * t_one.astype(f32) + polyak_rate * q_one.astype(f32)).astype(
        bf16
    )
    new_two = ((1.0 - polyak_rate) * t_two.astype(f32) + polyak_rate * q_two.astype(f32)).astype(
        bf16
    )
    return (loss, head_one, head_two, value_grad, bias_grad.reshape(1), new_one, new_two)


def solution(mesh):
    in_specs = (
        P("dp", None, "mp"),
        P("dp", None),
        P("dp", None),
        P("dp"),
        P("dp", "mp"),
        P("dp", "mp"),
        P("dp", "mp"),
        P("dp", "mp"),
        P("dp", "mp"),
        P("mp"),
        P(),
    )
    out_specs = (P(), P("dp", "mp"), P("dp", "mp"), P("mp"), P(), P("dp", "mp"), P("dp", "mp"))
    return jax.shard_map(
        on_device, mesh=mesh, in_specs=in_specs, out_specs=out_specs, check_vma=False
    )
```

```python
import functools

import jax
import jax.numpy as jnp
from jax import lax
from jax.experimental import pallas as pl
from jax.experimental.pallas import tpu as pltpu
from jax.sharding import PartitionSpec as P

discount = 0.99
expectile = 0.7
polyak_rate = 0.005
f32 = jnp.float32
bf16 = jnp.bfloat16


def head_gelu(inputs):
    return jax.nn.gelu(inputs, approximate=True)


def slope(preact, upstream):
    _, pullback = jax.vjp(head_gelu, preact)
    return pullback(upstream)[0]


MESH = pl.DeviceIdType.MESH


def reduce_kernel(
    dp, mp, held, seat, found, w_one, w_two, w_three, w_four, goal, worth,
    back_out, score_out, value_out,
    send_y, recv_y, sums, send_z, recv_z, pre, board, scores, backs, grads,
    y_send, y_recv, z_send, z_recv, m_send, m_recv, s_send, s_recv, g_send, g_recv,
    dz_send, dz_recv, dy_send, dy_recv,
):
    me = lax.axis_index("dp")
    mine = lax.axis_index("mp")
    half = dp // 2
    z = lax.div(me, 2)
    y = lax.rem(me, 2)
    partner = z * 2 + (1 - y)
    packed = held.shape[0]
    share = packed // dp
    side = half * share
    cols = w_one.shape[1]
    block = y * half + z
    barrier = pltpu.get_barrier_semaphore()
    for r in range(1, dp):
        pl.semaphore_signal(
            barrier, inc=1, device_id={"dp": lax.rem(me + r, dp)}, device_id_type=MESH
        )
    for r in range(1, mp):
        pl.semaphore_signal(
            barrier, inc=1, device_id={"mp": lax.rem(mine + r, mp)}, device_id_type=MESH
        )
    pl.semaphore_wait(barrier, dp + mp - 2)

    def send(src, dst, one, two, axis, where):
        copy = pltpu.make_async_remote_copy(
            src_ref=src, dst_ref=dst, send_sem=one, recv_sem=two,
            device_id={axis: where}, device_id_type=MESH,
        )
        copy.start()
        return copy

    theirs = pl.ds(pl.multiple_of((1 - y) * side, side), side)
    ours = pl.ds(pl.multiple_of(y * side, side), side)
    factors = ((seat, found), (held, w_one), (held, w_two), (held, w_three), (held, w_four))
    tile = 128
    y_copies = []
    for k, (left, right) in enumerate(factors):

        @pl.loop(0, cols // tile)
        def _(c):
            at = pl.ds(pl.multiple_of(c * tile, tile), tile)
            send_y[k, :, at] = jnp.dot(
                left[theirs, :], right[:, at], preferred_element_type=f32
            ).astype(bf16)

        y_copies.append(
            send(send_y.at[k], recv_y.at[k], y_send.at[k], y_recv.at[k], "dp", partner)
        )

        @pl.loop(0, cols // tile)
        def _(c):
            at = pl.ds(pl.multiple_of(c * tile, tile), tile)
            sums[k, :, at] = jnp.dot(left[ours, :], right[:, at], preferred_element_type=f32)

    z_copies = []
    for k in range(5):
        y_copies[k].wait()

        @pl.loop(0, half)
        def _(h):
            at = pl.ds(pl.multiple_of(h * share, share), share)
            total = sums[k, at, :] + recv_y[k, at, :].astype(f32)
            sums[k, at, :] = total
            send_z[k, h] = total.astype(bf16)

        for r in range(1, half):
            to = lax.rem(z + r, half)
            z_copies.append(
                send(
                    send_z.at[k, to], recv_z.at[k, r - 1], z_send.at[k, r - 1],
                    z_recv.at[k, r - 1], "dp", to * 2 + y,
                )
            )
    lane = lax.broadcasted_iota(jnp.int32, (share, 128), 1)
    mine_at = pl.ds(pl.multiple_of(z * share, share), share)
    marks = jnp.zeros((share, 128), f32)
    for k in range(5):
        total = sums[k, mine_at, :]
        for r in range(1, half):
            z_copies[k * (half - 1) + r - 1].wait()
            total = total + recv_z[k, r - 1].astype(f32)
        pre[k] = total
        if k > 0:
            score = jnp.sum(head_gelu(total) * pre[0], axis=1, keepdims=True)
            marks = jnp.where(lane == k - 1, score, marks)
    board[mine] = marks
    m_copies = [
        send(
            board.at[mine], board.at[mine], m_send.at[r - 1], m_recv.at[r - 1], "mp",
            lax.rem(mine + r, mp),
        )
        for r in range(1, mp)
    ]
    for copy in m_copies:
        copy.wait()
    full = board[0]
    for r in range(1, mp):
        full = full + board[r]
    scores[block] = full
    s_copies = [
        send(
            scores.at[block], scores.at[block], s_send.at[r - 1], s_recv.at[r - 1], "dp",
            lax.rem(me + r, dp),
        )
        for r in range(1, dp)
    ]
    own_goal = goal[pl.ds(pl.multiple_of(block * share, share), share), :]
    for k in range(2):
        up = 2.0 * (full[:, k : k + 1] - own_goal)
        backs[block, :, k * cols : (k + 1) * cols] = slope(pre[k + 1], up * pre[0]).astype(bf16)
    dz_copies = [
        send(
            backs.at[block], backs.at[block], dz_send.at[r - 1], dz_recv.at[r - 1], "dp",
            lax.rem(z + r, half) * 2 + y,
        )
        for r in range(1, half)
    ]
    dy_copies = [
        send(backs.at[block], backs.at[block], dy_send.at[0], dy_recv.at[0], "dp", partner)
    ]
    for copy in s_copies:
        copy.wait()
    grad = jnp.zeros((1, held.shape[1]), f32)
    for h in range(dp):
        at = slice(h * share, (h + 1) * share)
        gap = jnp.minimum(scores[h, :, 2:3], scores[h, :, 3:4]) - worth[at, :]
        weight = jnp.where(gap < 0.0, 1.0 - expectile, expectile)
        error = -2.0 * weight * gap
        grad = grad + jnp.sum(error * held[at, :].astype(f32), axis=0, keepdims=True)
    grads[me] = jnp.broadcast_to(grad, (8, held.shape[1]))
    g_copies = [
        send(
            grads.at[me], grads.at[me], g_send.at[r - 1], g_recv.at[r - 1], "dp",
            lax.rem(me + r, dp),
        )
        for r in range(1, dp)
    ]
    for r in range(1, half):
        dz_copies[r - 1].wait()
        seen = y * half + lax.rem(z + half - r, half)
        dy_copies.append(
            send(backs.at[seen], backs.at[seen], dy_send.at[r], dy_recv.at[r], "dp", partner)
        )
    for copy in g_copies:
        copy.wait()
    value_out[...] = grads[...]
    score_out[...] = scores[...]
    for copy in dy_copies:
        copy.wait()
    back_out[...] = backs[...]


def reduce_call(dp, mp, held, seat, found, weights, goal, worth):
    packed, rows = held.shape
    cols = weights[0].shape[1]
    half = dp // 2
    share = packed // dp
    side = share * half
    dma = pltpu.SemaphoreType.DMA
    vmem = pl.BlockSpec(memory_space=pltpu.VMEM)
    return pl.pallas_call(
        functools.partial(reduce_kernel, dp, mp),
        out_shape=(
            jax.ShapeDtypeStruct((dp, share, 2 * cols), bf16),
            jax.ShapeDtypeStruct((dp, share, 128), f32),
            jax.ShapeDtypeStruct((dp, 8, rows), f32),
        ),
        in_specs=[vmem] * 9,
        out_specs=(vmem, vmem, vmem),
        scratch_shapes=[
            pltpu.VMEM((5, side, cols), bf16),
            pltpu.VMEM((5, side, cols), bf16),
            pltpu.VMEM((5, side, cols), f32),
            pltpu.VMEM((5, half, share, cols), bf16),
            pltpu.VMEM((5, half - 1, share, cols), bf16),
            pltpu.VMEM((5, share, cols), f32),
            pltpu.VMEM((mp, share, 128), f32),
            pltpu.VMEM((dp, share, 128), f32),
            pltpu.VMEM((dp, share, 2 * cols), bf16),
            pltpu.VMEM((dp, 8, rows), f32),
            dma((5,)), dma((5,)), dma((5, half - 1)), dma((5, half - 1)),
            dma((mp - 1,)), dma((mp - 1,)), dma((dp - 1,)), dma((dp - 1,)),
            dma((dp - 1,)), dma((dp - 1,)), dma((half - 1,)), dma((half - 1,)),
            dma((half,)), dma((half,)),
        ],
        compiler_params=pltpu.CompilerParams(
            collective_id=1, has_side_effects=True, vmem_limit_bytes=56 << 20
        ),
    )(held, seat, found, *weights, goal, worth)


def pick(mask, row):
    return jnp.sum(jnp.where(mask, row[None, :], jnp.zeros((), row.dtype)), axis=1)


def on_device(
    hidden, rewards, actions, lengths, table, q_one, q_two, t_one, t_two, value_weight, value_bias
):
    dp = lax.axis_size("dp")
    me = lax.axis_index("dp")
    prompts, slots, width = hidden.shape
    own = prompts * slots
    total = own * dp
    packed = total // 2
    share = packed // dp
    cols = q_one.shape[1]
    rows = q_one.shape[0]
    local_rows = table.shape[0]
    local_flat = hidden.reshape(own, width)

    stacked = jnp.concatenate([local_flat, value_weight.reshape(1, width)], axis=0)
    wide = lax.all_gather(stacked, "mp", axis=1, tiled=True)
    flat, value_row = wide[:own], wide[own:]
    values = (
        jnp.sum(flat.astype(f32) * value_row.astype(f32), axis=1).reshape(prompts, slots)
        + value_bias[0]
    )
    positions = jnp.arange(slots, dtype=jnp.int32)[None, :]
    follows = positions + 1 < lengths[:, None]
    shifted = jnp.concatenate([values[:, 1:], jnp.zeros_like(values[:, :1])], axis=1)
    target = rewards + discount * jnp.where(follows, shifted, 0.0)

    ints = jnp.concatenate([actions, lengths[:, None]], axis=1)
    all_ints = lax.all_gather(ints, "dp", axis=0, tiled=True)
    all_lengths = all_ints[:, slots]
    ids = all_ints[:, :slots].reshape(total)
    facts = jnp.stack([target.reshape(own), values.reshape(own)])
    all_facts = lax.all_gather(facts, "dp", axis=1, tiled=True)
    count = jnp.sum(all_lengths).astype(f32)
    factor = 1.0 / count

    prompt_ids = jnp.arange(prompts * dp, dtype=jnp.int32)
    offsets = jnp.sum(
        jnp.where(prompt_ids[None, :] < prompt_ids[:, None], all_lengths[None, :], 0), axis=1
    )
    place = jnp.where(
        positions < all_lengths[:, None], offsets[:, None] + positions, -1
    ).reshape(total)
    own_slots = jnp.arange(share, dtype=jnp.int32)[:, None] + me * share
    own_mask = own_slots == place[None, :]

    holders = ids // local_rows
    by_source = holders.reshape(dp, own)
    order = jnp.arange(own, dtype=jnp.int32)
    earlier = (by_source[:, :, None] == by_source[:, None, :]) & (
        order[None, None, :] < order[None, :, None]
    )
    per_source = own // dp
    rank = (
        jnp.sum(earlier.astype(jnp.int32), axis=2)
        + jnp.arange(dp, dtype=jnp.int32)[:, None] * per_source
    ).reshape(total)
    where_held = holders * own + rank
    wanted = jnp.arange(own, dtype=jnp.int32)[:, None] + me * own == where_held[None, :]
    requests = pick(wanted, ids - me * local_rows)
    found = table[requests]

    spread = lax.all_to_all(flat, "dp", split_axis=1, concat_axis=0, tiled=True)
    pack_mask = (jnp.arange(packed, dtype=jnp.int32)[:, None] == place[None, :]).astype(bf16)
    held = jnp.dot(pack_mask, spread, preferred_element_type=f32).astype(bf16)

    pack_bool = jnp.arange(packed, dtype=jnp.int32)[:, None] == place[None, :]
    goal = pick(pack_bool, all_facts[0])
    worth = pick(pack_bool, all_facts[1])
    in_vmem = 30 * packed * cols < (32 << 20)
    if in_vmem:
        seats = pick(pack_bool, where_held) - me * own
        seat = (seats[:, None] == jnp.arange(own, dtype=jnp.int32)[None, :]).astype(bf16)
        backs, tiles, grads = reduce_call(
            dp, lax.axis_size("mp"), held, seat, found, (q_one, q_two, t_one, t_two),
            goal[:, None], worth[:, None],
        )
        all_scores = tiles.reshape(packed, 128)[:, :4].T
    else:
        all_found = lax.all_gather(found, "dp", axis=0, tiled=True)
        seat = pick(own_mask, where_held)
        seat_mask = (jnp.arange(total, dtype=jnp.int32)[None, :] == seat[:, None]).astype(bf16)
        embed = jnp.dot(seat_mask, all_found, preferred_element_type=f32)
        partial = jnp.concatenate(
            [
                jnp.dot(held, weight, preferred_element_type=f32).astype(bf16)
                for weight in (q_one, q_two, t_one, t_two)
            ],
            axis=1,
        )
        swapped = lax.all_to_all(partial, "dp", split_axis=0, concat_axis=0, tiled=True)
        pre = jnp.sum(swapped.reshape(dp, share, 4 * cols).astype(f32), axis=0)
        pres = [pre[:, k * cols : (k + 1) * cols] for k in range(4)]
        scores = jnp.stack([jnp.sum(head_gelu(p) * embed, axis=1) for p in pres])
        board = lax.dynamic_update_slice(
            jnp.zeros((4, packed), f32), scores, (jnp.zeros((), jnp.int32), me * share)
        )
        all_scores = lax.psum(board, ("dp", "mp"))

    lowest = jnp.minimum(all_scores[2], all_scores[3])
    spread_to = lowest - worth
    weights = jnp.where(spread_to < 0.0, 1.0 - expectile, expectile)
    err_one = all_scores[0] - goal
    err_two = all_scores[1] - goal
    loss = (
        jnp.sum(err_one * err_one + err_two * err_two + weights * spread_to * spread_to) * factor
    )
    grad_values = -2.0 * weights * spread_to
    bias_grad = jnp.sum(grad_values) * factor

    if in_vmem:
        all_back = backs.reshape(packed, 2 * cols)
    else:
        up_one = lax.dynamic_slice(2.0 * err_one, (me * share,), (share,))
        up_two = lax.dynamic_slice(2.0 * err_two, (me * share,), (share,))
        back = jnp.concatenate(
            [
                slope(pres[0], up_one[:, None] * embed).astype(bf16),
                slope(pres[1], up_two[:, None] * embed).astype(bf16),
            ],
            axis=1,
        )
        all_back = lax.all_gather(back, "dp", axis=0, tiled=True)
    dims = (((0,), (0,)), ((), ()))
    head_one = (
        lax.dot_general(held, all_back[:, :cols], dims, preferred_element_type=f32) * factor
    )
    head_two = (
        lax.dot_general(held, all_back[:, cols:], dims, preferred_element_type=f32) * factor
    )

    if in_vmem:
        features = grads[:, 0, :].reshape(dp * rows)
        value_grad = (
            lax.dynamic_slice(features, (lax.axis_index("mp") * width,), (width,)) * factor
        )
    else:
        own_place = lax.dynamic_slice(place, (me * own,), (own,))
        own_errors = pick(
            own_place[:, None] == jnp.arange(packed, dtype=jnp.int32)[None, :], grad_values
        )
        value_part = jnp.sum(own_errors[:, None] * local_flat.astype(f32), axis=0)
        value_grad = lax.psum(value_part * factor, "dp")
    new_one = ((1.0 - polyak_rate) * t_one.astype(f32) + polyak_rate * q_one.astype(f32)).astype(
        bf16
    )
    new_two = ((1.0 - polyak_rate) * t_two.astype(f32) + polyak_rate * q_two.astype(f32)).astype(
        bf16
    )
    return (loss, head_one, head_two, value_grad, bias_grad.reshape(1), new_one, new_two)


def solution(mesh):
    in_specs = (
        P("dp", None, "mp"),
        P("dp", None),
        P("dp", None),
        P("dp"),
        P("dp", "mp"),
        P("dp", "mp"),
        P("dp", "mp"),
        P("dp", "mp"),
        P("dp", "mp"),
        P("mp"),
        P(),
    )
    out_specs = (P(), P("dp", "mp"), P("dp", "mp"), P("mp"), P(), P("dp", "mp"), P("dp", "mp"))
    return jax.shard_map(
        on_device, mesh=mesh, in_specs=in_specs, out_specs=out_specs, check_vma=False
    )
```

```python
import functools

import jax
import jax.numpy as jnp
from jax import lax
from jax.experimental import pallas as pl
from jax.experimental.pallas import tpu as pltpu
from jax.sharding import PartitionSpec as P

discount = 0.99
expectile = 0.7
polyak_rate = 0.005
f32 = jnp.float32
bf16 = jnp.bfloat16


def head_gelu(inputs):
    return jax.nn.gelu(inputs, approximate=True)


def slope(preact, upstream):
    _, pullback = jax.vjp(head_gelu, preact)
    return pullback(upstream)[0]


MESH = pl.DeviceIdType.MESH


def reduce_kernel(
    dp, mp, held, seat, found, w_one, w_two, w_three, w_four, goal, worth,
    back_out, score_out, value_out,
    send_y, recv_y, sums, send_z, recv_z, pre, board, scores, backs, grads,
    y_send, y_recv, z_send, z_recv, m_send, m_recv, s_send, s_recv, g_send, g_recv,
    dz_send, dz_recv, dy_send, dy_recv,
):
    me = lax.axis_index("dp")
    mine = lax.axis_index("mp")
    half = dp // 2
    z = lax.div(me, 2)
    y = lax.rem(me, 2)
    partner = z * 2 + (1 - y)
    packed = held.shape[0]
    share = packed // dp
    side = half * share
    cols = w_one.shape[1]
    block = y * half + z
    barrier = pltpu.get_barrier_semaphore()
    for r in range(1, dp):
        pl.semaphore_signal(
            barrier, inc=1, device_id={"dp": lax.rem(me + r, dp)}, device_id_type=MESH
        )
    for r in range(1, mp):
        pl.semaphore_signal(
            barrier, inc=1, device_id={"mp": lax.rem(mine + r, mp)}, device_id_type=MESH
        )
    pl.semaphore_wait(barrier, dp + mp - 2)

    def send(src, dst, one, two, axis, where):
        copy = pltpu.make_async_remote_copy(
            src_ref=src, dst_ref=dst, send_sem=one, recv_sem=two,
            device_id={axis: where}, device_id_type=MESH,
        )
        copy.start()
        return copy

    theirs = pl.ds(pl.multiple_of((1 - y) * side, side), side)
    ours = pl.ds(pl.multiple_of(y * side, side), side)
    factors = ((seat, found), (held, w_one), (held, w_two), (held, w_three), (held, w_four))
    tile = 128
    y_copies = []
    for k, (left, right) in enumerate(factors):

        @pl.loop(0, cols // tile)
        def _(c):
            at = pl.ds(pl.multiple_of(c * tile, tile), tile)
            send_y[k, :, at] = jnp.dot(
                left[theirs, :], right[:, at], preferred_element_type=f32
            ).astype(bf16)

        y_copies.append(
            send(send_y.at[k], recv_y.at[k], y_send.at[k], y_recv.at[k], "dp", partner)
        )

        @pl.loop(0, cols // tile)
        def _(c):
            at = pl.ds(pl.multiple_of(c * tile, tile), tile)
            sums[k, :, at] = jnp.dot(left[ours, :], right[:, at], preferred_element_type=f32)

    z_copies = {}

    def along_z(k):
        y_copies[k].wait()

        @pl.loop(0, half)
        def _(h):
            at = pl.ds(pl.multiple_of(h * share, share), share)
            total = sums[k, at, :] + recv_y[k, at, :].astype(f32)
            sums[k, at, :] = total
            send_z[k, h] = total.astype(bf16)

        z_copies[k] = []
        for r in range(1, half):
            to = lax.rem(z + r, half)
            z_copies[k].append(
                send(
                    send_z.at[k, to], recv_z.at[k, r - 1], z_send.at[k, r - 1],
                    z_recv.at[k, r - 1], "dp", to * 2 + y,
                )
            )

    lane = lax.broadcasted_iota(jnp.int32, (share, 128), 1)
    mine_at = pl.ds(pl.multiple_of(z * share, share), share)

    def finish(k):
        total = sums[k, mine_at, :]
        for r in range(1, half):
            z_copies[k][r - 1].wait()
            total = total + recv_z[k, r - 1].astype(f32)
        pre[k] = total

    def over_mp(pair, first):
        marks = jnp.zeros((share, 128), f32)
        for k in (first, first + 1):
            finish(k)
            score = jnp.sum(head_gelu(pre[k]) * pre[0], axis=1, keepdims=True)
            marks = jnp.where(lane == k - 1, score, marks)
        board[pair, mine] = marks
        m_copies = [
            send(
                board.at[pair, mine], board.at[pair, mine], m_send.at[pair, r - 1],
                m_recv.at[pair, r - 1], "mp", lax.rem(mine + r, mp),
            )
            for r in range(1, mp)
        ]
        for copy in m_copies:
            copy.wait()
        full = board[pair, 0]
        for r in range(1, mp):
            full = full + board[pair, r]
        return full

    for k in range(4):
        along_z(k)
    finish(0)
    full = over_mp(0, 1)
    own_goal = goal[pl.ds(pl.multiple_of(block * share, share), share), :]
    for k in range(2):
        up = 2.0 * (full[:, k : k + 1] - own_goal)
        backs[block, :, k * cols : (k + 1) * cols] = slope(pre[k + 1], up * pre[0]).astype(bf16)
    along_z(4)
    dz_copies = [
        send(
            backs.at[block], backs.at[block], dz_send.at[r - 1], dz_recv.at[r - 1], "dp",
            lax.rem(z + r, half) * 2 + y,
        )
        for r in range(1, half)
    ]
    dy_copies = [
        send(backs.at[block], backs.at[block], dy_send.at[0], dy_recv.at[0], "dp", partner)
    ]
    full = full + over_mp(1, 3)
    scores[block] = full
    s_copies = [
        send(
            scores.at[block], scores.at[block], s_send.at[r - 1], s_recv.at[r - 1], "dp",
            lax.rem(me + r, dp),
        )
        for r in range(1, dp)
    ]
    for r in range(1, half):
        dz_copies[r - 1].wait()
        seen = y * half + lax.rem(z + half - r, half)
        dy_copies.append(
            send(backs.at[seen], backs.at[seen], dy_send.at[r], dy_recv.at[r], "dp", partner)
        )
    for copy in s_copies:
        copy.wait()
    grad = jnp.zeros((1, held.shape[1]), f32)
    for h in range(dp):
        at = slice(h * share, (h + 1) * share)
        gap = jnp.minimum(scores[h, :, 2:3], scores[h, :, 3:4]) - worth[at, :]
        weight = jnp.where(gap < 0.0, 1.0 - expectile, expectile)
        error = -2.0 * weight * gap
        grad = grad + jnp.sum(error * held[at, :].astype(f32), axis=0, keepdims=True)
    grads[me] = jnp.broadcast_to(grad, (8, held.shape[1]))
    g_copies = [
        send(
            grads.at[me], grads.at[me], g_send.at[r - 1], g_recv.at[r - 1], "dp",
            lax.rem(me + r, dp),
        )
        for r in range(1, dp)
    ]
    for copy in g_copies:
        copy.wait()
    value_out[...] = grads[...]
    score_out[...] = scores[...]
    for copy in dy_copies:
        copy.wait()
    back_out[...] = backs[...]


def reduce_call(dp, mp, held, seat, found, weights, goal, worth):
    packed, rows = held.shape
    cols = weights[0].shape[1]
    half = dp // 2
    share = packed // dp
    side = share * half
    dma = pltpu.SemaphoreType.DMA
    vmem = pl.BlockSpec(memory_space=pltpu.VMEM)
    return pl.pallas_call(
        functools.partial(reduce_kernel, dp, mp),
        out_shape=(
            jax.ShapeDtypeStruct((dp, share, 2 * cols), bf16),
            jax.ShapeDtypeStruct((dp, share, 128), f32),
            jax.ShapeDtypeStruct((dp, 8, rows), f32),
        ),
        in_specs=[vmem] * 9,
        out_specs=(vmem, vmem, vmem),
        scratch_shapes=[
            pltpu.VMEM((5, side, cols), bf16),
            pltpu.VMEM((5, side, cols), bf16),
            pltpu.VMEM((5, side, cols), f32),
            pltpu.VMEM((5, half, share, cols), bf16),
            pltpu.VMEM((5, half - 1, share, cols), bf16),
            pltpu.VMEM((5, share, cols), f32),
            pltpu.VMEM((2, mp, share, 128), f32),
            pltpu.VMEM((dp, share, 128), f32),
            pltpu.VMEM((dp, share, 2 * cols), bf16),
            pltpu.VMEM((dp, 8, rows), f32),
            dma((5,)), dma((5,)), dma((5, half - 1)), dma((5, half - 1)),
            dma((2, mp - 1)), dma((2, mp - 1)), dma((dp - 1,)), dma((dp - 1,)),
            dma((dp - 1,)), dma((dp - 1,)), dma((half - 1,)), dma((half - 1,)),
            dma((half,)), dma((half,)),
        ],
        compiler_params=pltpu.CompilerParams(
            collective_id=1, has_side_effects=True, vmem_limit_bytes=56 << 20
        ),
    )(held, seat, found, *weights, goal, worth)


def spread_kernel(
    dp, mp, hid, ints, rewards, parts,
    hid_out, int_out, float_out,
    wide, landed, marks, sums, facts,
    a_send, a_recv, b_send, b_recv, i_send, i_recv, v_send, v_recv, f_send, f_recv,
):
    me = lax.axis_index("dp")
    mine = lax.axis_index("mp")
    per = dp // mp
    barrier = pltpu.get_barrier_semaphore()
    for r in range(1, dp):
        pl.semaphore_signal(
            barrier, inc=1, device_id={"dp": lax.rem(me + r, dp)}, device_id_type=MESH
        )
    for r in range(1, mp):
        pl.semaphore_signal(
            barrier, inc=1, device_id={"mp": lax.rem(mine + r, mp)}, device_id_type=MESH
        )
    pl.semaphore_wait(barrier, dp + mp - 2)

    def send(src, dst, one, two, axis, where):
        copy = pltpu.make_async_remote_copy(
            src_ref=src, dst_ref=dst, send_sem=one, recv_sem=two,
            device_id={axis: where}, device_id_type=MESH,
        )
        copy.start()
        return copy

    blocks = pl.ds(mine * per, per)
    v_copies = [
        send(
            parts, sums.at[mine], v_send.at[r - 1], v_recv.at[r - 1], "mp", lax.rem(mine + r, mp)
        )
        for r in range(1, mp)
    ]
    a_copies = [
        send(
            hid, wide.at[blocks], a_send.at[r - 1], a_recv.at[r - 1], "mp", lax.rem(mine + r, mp)
        )
        for r in range(1, mp)
    ]
    i_copies = [
        send(ints, marks.at[me], i_send.at[r - 1], i_recv.at[r - 1], "dp", lax.rem(me + r, dp))
        for r in range(1, dp)
    ]
    wide[blocks] = hid[...]
    sums[mine] = parts[...]
    marks[me] = ints[...]
    for copy in v_copies:
        copy.wait()
    total = sums[0]
    for r in range(1, mp):
        total = total + sums[r]
    row = lax.broadcasted_iota(jnp.int32, total.shape, 0)
    facts[me] = jnp.where(row == 0, rewards[...], total)
    for copy in a_copies:
        copy.wait()
    b_copies = []
    for r in range(1, dp):
        to = lax.rem(me + r, dp)
        b_copies.append(
            send(wide.at[to], landed.at[me], b_send.at[r - 1], b_recv.at[r - 1], "dp", to)
        )
    f_copies = [
        send(facts.at[me], facts.at[me], f_send.at[r - 1], f_recv.at[r - 1], "dp", lax.rem(me + r, dp))
        for r in range(1, dp)
    ]
    landed[me] = wide[me]
    for copy in i_copies:
        copy.wait()
    int_out[...] = marks[...]
    for copy in f_copies:
        copy.wait()
    float_out[...] = facts[...]
    for copy in b_copies:
        copy.wait()
    hid_out[...] = landed[...]


def spread_call(dp, mp, hid, ints, rewards, parts):
    dma = pltpu.SemaphoreType.DMA
    vmem = pl.BlockSpec(memory_space=pltpu.VMEM)
    shape = (dp,) + hid.shape[1:]
    return pl.pallas_call(
        functools.partial(spread_kernel, dp, mp),
        out_shape=(
            jax.ShapeDtypeStruct(shape, bf16),
            jax.ShapeDtypeStruct((dp,) + ints.shape, jnp.int32),
            jax.ShapeDtypeStruct((dp,) + parts.shape, f32),
        ),
        in_specs=[vmem] * 4,
        out_specs=(vmem, vmem, vmem),
        scratch_shapes=[
            pltpu.VMEM(shape, bf16),
            pltpu.VMEM(shape, bf16),
            pltpu.VMEM((dp,) + ints.shape, jnp.int32),
            pltpu.VMEM((mp,) + parts.shape, f32),
            pltpu.VMEM((dp,) + parts.shape, f32),
            dma((mp - 1,)), dma((mp - 1,)), dma((dp - 1,)), dma((dp - 1,)),
            dma((dp - 1,)), dma((dp - 1,)), dma((mp - 1,)), dma((mp - 1,)),
            dma((dp - 1,)), dma((dp - 1,)),
        ],
        compiler_params=pltpu.CompilerParams(
            collective_id=2, has_side_effects=True, vmem_limit_bytes=24 << 20
        ),
    )(hid, ints, rewards, parts)


def pick(mask, row):
    return jnp.sum(jnp.where(mask, row[None, :], jnp.zeros((), row.dtype)), axis=1)


def on_device(
    hidden, rewards, actions, lengths, table, q_one, q_two, t_one, t_two, value_weight, value_bias
):
    dp = lax.axis_size("dp")
    me = lax.axis_index("dp")
    prompts, slots, width = hidden.shape
    own = prompts * slots
    total = own * dp
    packed = total // 2
    share = packed // dp
    cols = q_one.shape[1]
    rows = q_one.shape[0]
    local_rows = table.shape[0]
    local_flat = hidden.reshape(own, width)

    positions = jnp.arange(slots, dtype=jnp.int32)[None, :]
    mp = lax.axis_size("mp")
    in_vmem = 30 * packed * cols < (32 << 20) and dp % mp == 0 and slots >= prompts
    if in_vmem:
        hid = jnp.transpose(local_flat.reshape(own, dp // mp, rows), (1, 0, 2))
        part = jnp.sum(local_flat.astype(f32) * value_weight.astype(f32)[None, :], axis=1)
        ints = jnp.zeros((8, own), jnp.int32)
        ints = ints.at[0].set(actions.reshape(own)).at[1, :prompts].set(lengths)
        pages, int_tiles, fact_tiles = spread_call(
            dp, mp, hid, ints, jnp.broadcast_to(rewards.reshape(1, own), (8, own)),
            jnp.broadcast_to(part[None, :], (8, own)),
        )
        spread = pages.reshape(total, rows)
        ids = int_tiles[:, 0].reshape(total)
        all_lengths = int_tiles[:, 1, :prompts].reshape(prompts * dp)
        all_values = fact_tiles[:, 1].reshape(prompts * dp, slots) + value_bias[0]
        all_rewards = fact_tiles[:, 0].reshape(prompts * dp, slots)
        follows = positions + 1 < all_lengths[:, None]
        shifted = jnp.concatenate([all_values[:, 1:], jnp.zeros_like(all_values[:, :1])], axis=1)
        all_targets = all_rewards + discount * jnp.where(follows, shifted, 0.0)
        all_facts = jnp.stack([all_targets.reshape(total), all_values.reshape(total)])
    else:
        stacked = jnp.concatenate([local_flat, value_weight.reshape(1, width)], axis=0)
        wide = lax.all_gather(stacked, "mp", axis=1, tiled=True)
        flat, value_row = wide[:own], wide[own:]
        values = (
            jnp.sum(flat.astype(f32) * value_row.astype(f32), axis=1).reshape(prompts, slots)
            + value_bias[0]
        )
        follows = positions + 1 < lengths[:, None]
        shifted = jnp.concatenate([values[:, 1:], jnp.zeros_like(values[:, :1])], axis=1)
        target = rewards + discount * jnp.where(follows, shifted, 0.0)

        ints = jnp.concatenate([actions, lengths[:, None]], axis=1)
        all_ints = lax.all_gather(ints, "dp", axis=0, tiled=True)
        all_lengths = all_ints[:, slots]
        ids = all_ints[:, :slots].reshape(total)
        facts = jnp.stack([target.reshape(own), values.reshape(own)])
        all_facts = lax.all_gather(facts, "dp", axis=1, tiled=True)
        spread = lax.all_to_all(flat, "dp", split_axis=1, concat_axis=0, tiled=True)
    count = jnp.sum(all_lengths).astype(f32)
    factor = 1.0 / count

    prompt_ids = jnp.arange(prompts * dp, dtype=jnp.int32)
    offsets = jnp.sum(
        jnp.where(prompt_ids[None, :] < prompt_ids[:, None], all_lengths[None, :], 0), axis=1
    )
    place = jnp.where(
        positions < all_lengths[:, None], offsets[:, None] + positions, -1
    ).reshape(total)
    own_slots = jnp.arange(share, dtype=jnp.int32)[:, None] + me * share
    own_mask = own_slots == place[None, :]

    holders = ids // local_rows
    by_source = holders.reshape(dp, own)
    order = jnp.arange(own, dtype=jnp.int32)
    earlier = (by_source[:, :, None] == by_source[:, None, :]) & (
        order[None, None, :] < order[None, :, None]
    )
    per_source = own // dp
    rank = (
        jnp.sum(earlier.astype(jnp.int32), axis=2)
        + jnp.arange(dp, dtype=jnp.int32)[:, None] * per_source
    ).reshape(total)
    where_held = holders * own + rank
    wanted = jnp.arange(own, dtype=jnp.int32)[:, None] + me * own == where_held[None, :]
    requests = pick(wanted, ids - me * local_rows)
    found = table[requests]

    pack_mask = (jnp.arange(packed, dtype=jnp.int32)[:, None] == place[None, :]).astype(bf16)
    held = jnp.dot(pack_mask, spread, preferred_element_type=f32).astype(bf16)

    pack_bool = jnp.arange(packed, dtype=jnp.int32)[:, None] == place[None, :]
    goal = pick(pack_bool, all_facts[0])
    worth = pick(pack_bool, all_facts[1])
    if in_vmem:
        seats = pick(pack_bool, where_held) - me * own
        seat = (seats[:, None] == jnp.arange(own, dtype=jnp.int32)[None, :]).astype(bf16)
        backs, tiles, grads = reduce_call(
            dp, lax.axis_size("mp"), held, seat, found, (q_one, q_two, t_one, t_two),
            goal[:, None], worth[:, None],
        )
        all_scores = tiles.reshape(packed, 128)[:, :4].T
    else:
        all_found = lax.all_gather(found, "dp", axis=0, tiled=True)
        seat = pick(own_mask, where_held)
        seat_mask = (jnp.arange(total, dtype=jnp.int32)[None, :] == seat[:, None]).astype(bf16)
        embed = jnp.dot(seat_mask, all_found, preferred_element_type=f32)
        partial = jnp.concatenate(
            [
                jnp.dot(held, weight, preferred_element_type=f32).astype(bf16)
                for weight in (q_one, q_two, t_one, t_two)
            ],
            axis=1,
        )
        swapped = lax.all_to_all(partial, "dp", split_axis=0, concat_axis=0, tiled=True)
        pre = jnp.sum(swapped.reshape(dp, share, 4 * cols).astype(f32), axis=0)
        pres = [pre[:, k * cols : (k + 1) * cols] for k in range(4)]
        scores = jnp.stack([jnp.sum(head_gelu(p) * embed, axis=1) for p in pres])
        board = lax.dynamic_update_slice(
            jnp.zeros((4, packed), f32), scores, (jnp.zeros((), jnp.int32), me * share)
        )
        all_scores = lax.psum(board, ("dp", "mp"))

    lowest = jnp.minimum(all_scores[2], all_scores[3])
    spread_to = lowest - worth
    weights = jnp.where(spread_to < 0.0, 1.0 - expectile, expectile)
    err_one = all_scores[0] - goal
    err_two = all_scores[1] - goal
    loss = (
        jnp.sum(err_one * err_one + err_two * err_two + weights * spread_to * spread_to) * factor
    )
    grad_values = -2.0 * weights * spread_to
    bias_grad = jnp.sum(grad_values) * factor

    if in_vmem:
        all_back = backs.reshape(packed, 2 * cols)
    else:
        up_one = lax.dynamic_slice(2.0 * err_one, (me * share,), (share,))
        up_two = lax.dynamic_slice(2.0 * err_two, (me * share,), (share,))
        back = jnp.concatenate(
            [
                slope(pres[0], up_one[:, None] * embed).astype(bf16),
                slope(pres[1], up_two[:, None] * embed).astype(bf16),
            ],
            axis=1,
        )
        all_back = lax.all_gather(back, "dp", axis=0, tiled=True)
    dims = (((0,), (0,)), ((), ()))
    head_one = (
        lax.dot_general(held, all_back[:, :cols], dims, preferred_element_type=f32) * factor
    )
    head_two = (
        lax.dot_general(held, all_back[:, cols:], dims, preferred_element_type=f32) * factor
    )

    if in_vmem:
        features = grads[:, 0, :].reshape(dp * rows)
        value_grad = (
            lax.dynamic_slice(features, (lax.axis_index("mp") * width,), (width,)) * factor
        )
    else:
        own_place = lax.dynamic_slice(place, (me * own,), (own,))
        own_errors = pick(
            own_place[:, None] == jnp.arange(packed, dtype=jnp.int32)[None, :], grad_values
        )
        value_part = jnp.sum(own_errors[:, None] * local_flat.astype(f32), axis=0)
        value_grad = lax.psum(value_part * factor, "dp")
    new_one = ((1.0 - polyak_rate) * t_one.astype(f32) + polyak_rate * q_one.astype(f32)).astype(
        bf16
    )
    new_two = ((1.0 - polyak_rate) * t_two.astype(f32) + polyak_rate * q_two.astype(f32)).astype(
        bf16
    )
    return (loss, head_one, head_two, value_grad, bias_grad.reshape(1), new_one, new_two)


def solution(mesh):
    in_specs = (
        P("dp", None, "mp"),
        P("dp", None),
        P("dp", None),
        P("dp"),
        P("dp", "mp"),
        P("dp", "mp"),
        P("dp", "mp"),
        P("dp", "mp"),
        P("dp", "mp"),
        P("mp"),
        P(),
    )
    out_specs = (P(), P("dp", "mp"), P("dp", "mp"), P("mp"), P(), P("dp", "mp"), P("dp", "mp"))
    return jax.shard_map(
        on_device, mesh=mesh, in_specs=in_specs, out_specs=out_specs, check_vma=False
    )
```

```python
import functools

import jax
import jax.numpy as jnp
from jax import lax
from jax.experimental import pallas as pl
from jax.experimental.pallas import tpu as pltpu
from jax.sharding import PartitionSpec as P

discount = 0.99
expectile = 0.7
polyak_rate = 0.005
f32 = jnp.float32
bf16 = jnp.bfloat16


def head_gelu(inputs):
    return jax.nn.gelu(inputs, approximate=True)


def slope(preact, upstream):
    _, pullback = jax.vjp(head_gelu, preact)
    return pullback(upstream)[0]


MESH = pl.DeviceIdType.MESH


def reduce_kernel(
    dp, mp, held, seat, found, w_one, w_two, w_three, w_four, goal, worth,
    back_out, score_out, value_out,
    send_y, recv_y, sums, send_z, recv_z, pre, board, scores, backs, grads,
    y_send, y_recv, z_send, z_recv, m_send, m_recv, s_send, s_recv, g_send, g_recv,
    dz_send, dz_recv, dy_send, dy_recv,
):
    me = lax.axis_index("dp")
    mine = lax.axis_index("mp")
    half = dp // 2
    z = lax.div(me, 2)
    y = lax.rem(me, 2)
    partner = z * 2 + (1 - y)
    packed = held.shape[0]
    share = packed // dp
    side = half * share
    cols = w_one.shape[1]
    block = y * half + z
    barrier = pltpu.get_barrier_semaphore()
    for r in range(1, dp):
        pl.semaphore_signal(
            barrier, inc=1, device_id={"dp": lax.rem(me + r, dp)}, device_id_type=MESH
        )
    for r in range(1, mp):
        pl.semaphore_signal(
            barrier, inc=1, device_id={"mp": lax.rem(mine + r, mp)}, device_id_type=MESH
        )
    pl.semaphore_wait(barrier, dp + mp - 2)

    def send(src, dst, one, two, axis, where):
        copy = pltpu.make_async_remote_copy(
            src_ref=src, dst_ref=dst, send_sem=one, recv_sem=two,
            device_id={axis: where}, device_id_type=MESH,
        )
        copy.start()
        return copy

    theirs = pl.ds(pl.multiple_of((1 - y) * side, side), side)
    ours = pl.ds(pl.multiple_of(y * side, side), side)
    factors = ((seat, found), (held, w_one), (held, w_two), (held, w_three), (held, w_four))
    tile = 128
    y_copies = []
    for k, (left, right) in enumerate(factors):

        @pl.loop(0, cols // tile)
        def _(c):
            at = pl.ds(pl.multiple_of(c * tile, tile), tile)
            send_y[k, :, at] = jnp.dot(
                left[theirs, :], right[:, at], preferred_element_type=f32
            ).astype(bf16)

        y_copies.append(
            send(send_y.at[k], recv_y.at[k], y_send.at[k], y_recv.at[k], "dp", partner)
        )

        @pl.loop(0, cols // tile)
        def _(c):
            at = pl.ds(pl.multiple_of(c * tile, tile), tile)
            sums[k, :, at] = jnp.dot(left[ours, :], right[:, at], preferred_element_type=f32)

    z_copies = {}

    def along_z(k):
        y_copies[k].wait()

        @pl.loop(0, half)
        def _(h):
            at = pl.ds(pl.multiple_of(h * share, share), share)
            total = sums[k, at, :] + recv_y[k, at, :].astype(f32)
            sums[k, at, :] = total
            send_z[k, h] = total.astype(bf16)

        z_copies[k] = []
        for r in range(1, half):
            to = lax.rem(z + r, half)
            z_copies[k].append(
                send(
                    send_z.at[k, to], recv_z.at[k, r - 1], z_send.at[k, r - 1],
                    z_recv.at[k, r - 1], "dp", to * 2 + y,
                )
            )

    lane = lax.broadcasted_iota(jnp.int32, (share, 128), 1)
    mine_at = pl.ds(pl.multiple_of(z * share, share), share)

    def finish(k):
        total = sums[k, mine_at, :]
        for r in range(1, half):
            z_copies[k][r - 1].wait()
            total = total + recv_z[k, r - 1].astype(f32)
        pre[k] = total

    def over_mp(pair, first):
        marks = jnp.zeros((share, 128), f32)
        for k in (first, first + 1):
            finish(k)
            score = jnp.sum(head_gelu(pre[k]) * pre[0], axis=1, keepdims=True)
            marks = jnp.where(lane == k - 1, score, marks)
        board[pair, mine] = marks
        m_copies = [
            send(
                board.at[pair, mine], board.at[pair, mine], m_send.at[pair, r - 1],
                m_recv.at[pair, r - 1], "mp", lax.rem(mine + r, mp),
            )
            for r in range(1, mp)
        ]
        for copy in m_copies:
            copy.wait()
        full = board[pair, 0]
        for r in range(1, mp):
            full = full + board[pair, r]
        return full

    for k in range(4):
        along_z(k)
    finish(0)
    full = over_mp(0, 1)
    own_goal = goal[pl.ds(pl.multiple_of(block * share, share), share), :]
    for k in range(2):
        up = 2.0 * (full[:, k : k + 1] - own_goal)
        backs[block, :, k * cols : (k + 1) * cols] = slope(pre[k + 1], up * pre[0]).astype(bf16)
    along_z(4)
    dz_copies = [
        send(
            backs.at[block], backs.at[block], dz_send.at[r - 1], dz_recv.at[r - 1], "dp",
            lax.rem(z + r, half) * 2 + y,
        )
        for r in range(1, half)
    ]
    dy_copies = [
        send(backs.at[block], backs.at[block], dy_send.at[0], dy_recv.at[0], "dp", partner)
    ]
    full = full + over_mp(1, 3)
    scores[block] = full
    s_copies = [
        send(
            scores.at[block], scores.at[block], s_send.at[r - 1], s_recv.at[r - 1], "dp",
            lax.rem(me + r, dp),
        )
        for r in range(1, dp)
    ]
    for r in range(1, half):
        dz_copies[r - 1].wait()
        seen = y * half + lax.rem(z + half - r, half)
        dy_copies.append(
            send(backs.at[seen], backs.at[seen], dy_send.at[r], dy_recv.at[r], "dp", partner)
        )
    for copy in s_copies:
        copy.wait()
    grad = jnp.zeros((1, held.shape[1]), f32)
    for h in range(dp):
        at = slice(h * share, (h + 1) * share)
        gap = jnp.minimum(scores[h, :, 2:3], scores[h, :, 3:4]) - worth[at, :]
        weight = jnp.where(gap < 0.0, 1.0 - expectile, expectile)
        error = -2.0 * weight * gap
        grad = grad + jnp.sum(error * held[at, :].astype(f32), axis=0, keepdims=True)
    grads[me] = jnp.broadcast_to(grad, (8, held.shape[1]))
    g_copies = [
        send(
            grads.at[me], grads.at[me], g_send.at[r - 1], g_recv.at[r - 1], "dp",
            lax.rem(me + r, dp),
        )
        for r in range(1, dp)
    ]
    for copy in g_copies:
        copy.wait()
    value_out[...] = grads[...]
    score_out[...] = scores[...]
    for copy in dy_copies:
        copy.wait()
    back_out[...] = backs[...]


def reduce_call(dp, mp, held, seat, found, weights, goal, worth):
    packed, rows = held.shape
    cols = weights[0].shape[1]
    half = dp // 2
    share = packed // dp
    side = share * half
    dma = pltpu.SemaphoreType.DMA
    vmem = pl.BlockSpec(memory_space=pltpu.VMEM)
    return pl.pallas_call(
        functools.partial(reduce_kernel, dp, mp),
        out_shape=(
            jax.ShapeDtypeStruct((dp, share, 2 * cols), bf16),
            jax.ShapeDtypeStruct((dp, share, 128), f32),
            jax.ShapeDtypeStruct((dp, 8, rows), f32),
        ),
        in_specs=[vmem] * 9,
        out_specs=(vmem, vmem, vmem),
        scratch_shapes=[
            pltpu.VMEM((5, side, cols), bf16),
            pltpu.VMEM((5, side, cols), bf16),
            pltpu.VMEM((5, side, cols), f32),
            pltpu.VMEM((5, half, share, cols), bf16),
            pltpu.VMEM((5, half - 1, share, cols), bf16),
            pltpu.VMEM((5, share, cols), f32),
            pltpu.VMEM((2, mp, share, 128), f32),
            pltpu.VMEM((dp, share, 128), f32),
            pltpu.VMEM((dp, share, 2 * cols), bf16),
            pltpu.VMEM((dp, 8, rows), f32),
            dma((5,)), dma((5,)), dma((5, half - 1)), dma((5, half - 1)),
            dma((2, mp - 1)), dma((2, mp - 1)), dma((dp - 1,)), dma((dp - 1,)),
            dma((dp - 1,)), dma((dp - 1,)), dma((half - 1,)), dma((half - 1,)),
            dma((half,)), dma((half,)),
        ],
        compiler_params=pltpu.CompilerParams(
            collective_id=1, has_side_effects=True, vmem_limit_bytes=56 << 20
        ),
    )(held, seat, found, *weights, goal, worth)


def spread_kernel(
    dp, mp, hid, ints, rewards, parts,
    hid_out, int_out, float_out,
    wide, landed, marks, sums, facts,
    a_send, a_recv, b_send, b_recv, i_send, i_recv, v_send, v_recv, f_send, f_recv,
):
    me = lax.axis_index("dp")
    mine = lax.axis_index("mp")
    per = dp // mp
    barrier = pltpu.get_barrier_semaphore()
    for r in range(1, dp):
        pl.semaphore_signal(
            barrier, inc=1, device_id={"dp": lax.rem(me + r, dp)}, device_id_type=MESH
        )
    for r in range(1, mp):
        pl.semaphore_signal(
            barrier, inc=1, device_id={"mp": lax.rem(mine + r, mp)}, device_id_type=MESH
        )
    pl.semaphore_wait(barrier, dp + mp - 2)

    def send(src, dst, one, two, axis, where):
        copy = pltpu.make_async_remote_copy(
            src_ref=src, dst_ref=dst, send_sem=one, recv_sem=two,
            device_id={axis: where}, device_id_type=MESH,
        )
        copy.start()
        return copy

    blocks = pl.ds(mine * per, per)
    v_copies = [
        send(
            parts, sums.at[mine], v_send.at[r - 1], v_recv.at[r - 1], "mp", lax.rem(mine + r, mp)
        )
        for r in range(1, mp)
    ]
    a_copies = [
        send(
            hid, wide.at[blocks], a_send.at[r - 1], a_recv.at[r - 1], "mp", lax.rem(mine + r, mp)
        )
        for r in range(1, mp)
    ]
    i_copies = [
        send(ints, marks.at[me], i_send.at[r - 1], i_recv.at[r - 1], "dp", lax.rem(me + r, dp))
        for r in range(1, dp)
    ]
    wide[blocks] = hid[...]
    sums[mine] = parts[...]
    marks[me] = ints[...]
    for copy in v_copies:
        copy.wait()
    total = sums[0]
    for r in range(1, mp):
        total = total + sums[r]
    row = lax.broadcasted_iota(jnp.int32, total.shape, 0)
    facts[me] = jnp.where(row == 0, rewards[...], total)
    f_copies = [
        send(facts.at[me], facts.at[me], f_send.at[r - 1], f_recv.at[r - 1], "dp", lax.rem(me + r, dp))
        for r in range(1, dp)
    ]

    def across(to, r):
        return pltpu.make_async_remote_copy(
            src_ref=wide.at[to], dst_ref=landed.at[me], send_sem=b_send.at[r - 1],
            recv_sem=b_recv.at[r - 1], device_id={"dp": to}, device_id_type=MESH,
        )

    for step in range(mp):
        if step > 0:
            a_copies[step - 1].wait()
        for q in range(per):
            to = lax.rem(mine + mp - step, mp) * per + q

            @pl.when(to != me)
            def _():
                across(to, lax.rem(to - me + dp, dp)).start()

    landed[me] = wide[me]
    for copy in i_copies:
        copy.wait()
    int_out[...] = marks[...]
    for copy in f_copies:
        copy.wait()
    float_out[...] = facts[...]
    for r in range(1, dp):
        across(lax.rem(me + r, dp), r).wait()
    hid_out[...] = landed[...]


def spread_call(dp, mp, hid, ints, rewards, parts):
    dma = pltpu.SemaphoreType.DMA
    vmem = pl.BlockSpec(memory_space=pltpu.VMEM)
    shape = (dp,) + hid.shape[1:]
    return pl.pallas_call(
        functools.partial(spread_kernel, dp, mp),
        out_shape=(
            jax.ShapeDtypeStruct(shape, bf16),
            jax.ShapeDtypeStruct((dp,) + ints.shape, jnp.int32),
            jax.ShapeDtypeStruct((dp,) + parts.shape, f32),
        ),
        in_specs=[vmem] * 4,
        out_specs=(vmem, vmem, vmem),
        scratch_shapes=[
            pltpu.VMEM(shape, bf16),
            pltpu.VMEM(shape, bf16),
            pltpu.VMEM((dp,) + ints.shape, jnp.int32),
            pltpu.VMEM((mp,) + parts.shape, f32),
            pltpu.VMEM((dp,) + parts.shape, f32),
            dma((mp - 1,)), dma((mp - 1,)), dma((dp - 1,)), dma((dp - 1,)),
            dma((dp - 1,)), dma((dp - 1,)), dma((mp - 1,)), dma((mp - 1,)),
            dma((dp - 1,)), dma((dp - 1,)),
        ],
        compiler_params=pltpu.CompilerParams(
            collective_id=2, has_side_effects=True, vmem_limit_bytes=24 << 20
        ),
    )(hid, ints, rewards, parts)


def pick(mask, row):
    return jnp.sum(jnp.where(mask, row[None, :], jnp.zeros((), row.dtype)), axis=1)


def on_device(
    hidden, rewards, actions, lengths, table, q_one, q_two, t_one, t_two, value_weight, value_bias
):
    dp = lax.axis_size("dp")
    me = lax.axis_index("dp")
    prompts, slots, width = hidden.shape
    own = prompts * slots
    total = own * dp
    packed = total // 2
    share = packed // dp
    cols = q_one.shape[1]
    rows = q_one.shape[0]
    local_rows = table.shape[0]
    local_flat = hidden.reshape(own, width)

    positions = jnp.arange(slots, dtype=jnp.int32)[None, :]
    mp = lax.axis_size("mp")
    in_vmem = 30 * packed * cols < (32 << 20) and dp % mp == 0 and slots >= prompts
    if in_vmem:
        hid = jnp.transpose(local_flat.reshape(own, dp // mp, rows), (1, 0, 2))
        part = jnp.sum(local_flat.astype(f32) * value_weight.astype(f32)[None, :], axis=1)
        ints = jnp.zeros((8, own), jnp.int32)
        ints = ints.at[0].set(actions.reshape(own)).at[1, :prompts].set(lengths)
        pages, int_tiles, fact_tiles = spread_call(
            dp, mp, hid, ints, jnp.broadcast_to(rewards.reshape(1, own), (8, own)),
            jnp.broadcast_to(part[None, :], (8, own)),
        )
        spread = pages.reshape(total, rows)
        ids = int_tiles[:, 0].reshape(total)
        all_lengths = int_tiles[:, 1, :prompts].reshape(prompts * dp)
        all_values = fact_tiles[:, 1].reshape(prompts * dp, slots) + value_bias[0]
        all_rewards = fact_tiles[:, 0].reshape(prompts * dp, slots)
        follows = positions + 1 < all_lengths[:, None]
        shifted = jnp.concatenate([all_values[:, 1:], jnp.zeros_like(all_values[:, :1])], axis=1)
        all_targets = all_rewards + discount * jnp.where(follows, shifted, 0.0)
        all_facts = jnp.stack([all_targets.reshape(total), all_values.reshape(total)])
    else:
        stacked = jnp.concatenate([local_flat, value_weight.reshape(1, width)], axis=0)
        wide = lax.all_gather(stacked, "mp", axis=1, tiled=True)
        flat, value_row = wide[:own], wide[own:]
        values = (
            jnp.sum(flat.astype(f32) * value_row.astype(f32), axis=1).reshape(prompts, slots)
            + value_bias[0]
        )
        follows = positions + 1 < lengths[:, None]
        shifted = jnp.concatenate([values[:, 1:], jnp.zeros_like(values[:, :1])], axis=1)
        target = rewards + discount * jnp.where(follows, shifted, 0.0)

        ints = jnp.concatenate([actions, lengths[:, None]], axis=1)
        all_ints = lax.all_gather(ints, "dp", axis=0, tiled=True)
        all_lengths = all_ints[:, slots]
        ids = all_ints[:, :slots].reshape(total)
        facts = jnp.stack([target.reshape(own), values.reshape(own)])
        all_facts = lax.all_gather(facts, "dp", axis=1, tiled=True)
        spread = lax.all_to_all(flat, "dp", split_axis=1, concat_axis=0, tiled=True)
    count = jnp.sum(all_lengths).astype(f32)
    factor = 1.0 / count

    prompt_ids = jnp.arange(prompts * dp, dtype=jnp.int32)
    offsets = jnp.sum(
        jnp.where(prompt_ids[None, :] < prompt_ids[:, None], all_lengths[None, :], 0), axis=1
    )
    place = jnp.where(
        positions < all_lengths[:, None], offsets[:, None] + positions, -1
    ).reshape(total)
    own_slots = jnp.arange(share, dtype=jnp.int32)[:, None] + me * share
    own_mask = own_slots == place[None, :]

    holders = ids // local_rows
    by_source = holders.reshape(dp, own)
    order = jnp.arange(own, dtype=jnp.int32)
    earlier = (by_source[:, :, None] == by_source[:, None, :]) & (
        order[None, None, :] < order[None, :, None]
    )
    per_source = own // dp
    rank = (
        jnp.sum(earlier.astype(jnp.int32), axis=2)
        + jnp.arange(dp, dtype=jnp.int32)[:, None] * per_source
    ).reshape(total)
    where_held = holders * own + rank
    wanted = jnp.arange(own, dtype=jnp.int32)[:, None] + me * own == where_held[None, :]
    requests = pick(wanted, ids - me * local_rows)
    found = table[requests]

    pack_mask = (jnp.arange(packed, dtype=jnp.int32)[:, None] == place[None, :]).astype(bf16)
    held = jnp.dot(pack_mask, spread, preferred_element_type=f32).astype(bf16)

    pack_bool = jnp.arange(packed, dtype=jnp.int32)[:, None] == place[None, :]
    goal = pick(pack_bool, all_facts[0])
    worth = pick(pack_bool, all_facts[1])
    if in_vmem:
        seats = pick(pack_bool, where_held) - me * own
        seat = (seats[:, None] == jnp.arange(own, dtype=jnp.int32)[None, :]).astype(bf16)
        backs, tiles, grads = reduce_call(
            dp, lax.axis_size("mp"), held, seat, found, (q_one, q_two, t_one, t_two),
            goal[:, None], worth[:, None],
        )
        all_scores = tiles.reshape(packed, 128)[:, :4].T
    else:
        all_found = lax.all_gather(found, "dp", axis=0, tiled=True)
        seat = pick(own_mask, where_held)
        seat_mask = (jnp.arange(total, dtype=jnp.int32)[None, :] == seat[:, None]).astype(bf16)
        embed = jnp.dot(seat_mask, all_found, preferred_element_type=f32)
        partial = jnp.concatenate(
            [
                jnp.dot(held, weight, preferred_element_type=f32).astype(bf16)
                for weight in (q_one, q_two, t_one, t_two)
            ],
            axis=1,
        )
        swapped = lax.all_to_all(partial, "dp", split_axis=0, concat_axis=0, tiled=True)
        pre = jnp.sum(swapped.reshape(dp, share, 4 * cols).astype(f32), axis=0)
        pres = [pre[:, k * cols : (k + 1) * cols] for k in range(4)]
        scores = jnp.stack([jnp.sum(head_gelu(p) * embed, axis=1) for p in pres])
        board = lax.dynamic_update_slice(
            jnp.zeros((4, packed), f32), scores, (jnp.zeros((), jnp.int32), me * share)
        )
        all_scores = lax.psum(board, ("dp", "mp"))

    lowest = jnp.minimum(all_scores[2], all_scores[3])
    spread_to = lowest - worth
    weights = jnp.where(spread_to < 0.0, 1.0 - expectile, expectile)
    err_one = all_scores[0] - goal
    err_two = all_scores[1] - goal
    loss = (
        jnp.sum(err_one * err_one + err_two * err_two + weights * spread_to * spread_to) * factor
    )
    grad_values = -2.0 * weights * spread_to
    bias_grad = jnp.sum(grad_values) * factor

    if in_vmem:
        all_back = backs.reshape(packed, 2 * cols)
    else:
        up_one = lax.dynamic_slice(2.0 * err_one, (me * share,), (share,))
        up_two = lax.dynamic_slice(2.0 * err_two, (me * share,), (share,))
        back = jnp.concatenate(
            [
                slope(pres[0], up_one[:, None] * embed).astype(bf16),
                slope(pres[1], up_two[:, None] * embed).astype(bf16),
            ],
            axis=1,
        )
        all_back = lax.all_gather(back, "dp", axis=0, tiled=True)
    dims = (((0,), (0,)), ((), ()))
    head_one = (
        lax.dot_general(held, all_back[:, :cols], dims, preferred_element_type=f32) * factor
    )
    head_two = (
        lax.dot_general(held, all_back[:, cols:], dims, preferred_element_type=f32) * factor
    )

    if in_vmem:
        features = grads[:, 0, :].reshape(dp * rows)
        value_grad = (
            lax.dynamic_slice(features, (lax.axis_index("mp") * width,), (width,)) * factor
        )
    else:
        own_place = lax.dynamic_slice(place, (me * own,), (own,))
        own_errors = pick(
            own_place[:, None] == jnp.arange(packed, dtype=jnp.int32)[None, :], grad_values
        )
        value_part = jnp.sum(own_errors[:, None] * local_flat.astype(f32), axis=0)
        value_grad = lax.psum(value_part * factor, "dp")
    new_one = ((1.0 - polyak_rate) * t_one.astype(f32) + polyak_rate * q_one.astype(f32)).astype(
        bf16
    )
    new_two = ((1.0 - polyak_rate) * t_two.astype(f32) + polyak_rate * q_two.astype(f32)).astype(
        bf16
    )
    return (loss, head_one, head_two, value_grad, bias_grad.reshape(1), new_one, new_two)


def solution(mesh):
    in_specs = (
        P("dp", None, "mp"),
        P("dp", None),
        P("dp", None),
        P("dp"),
        P("dp", "mp"),
        P("dp", "mp"),
        P("dp", "mp"),
        P("dp", "mp"),
        P("dp", "mp"),
        P("mp"),
        P(),
    )
    out_specs = (P(), P("dp", "mp"), P("dp", "mp"), P("mp"), P(), P("dp", "mp"), P("dp", "mp"))
    return jax.shard_map(
        on_device, mesh=mesh, in_specs=in_specs, out_specs=out_specs, check_vma=False
    )
```
